32 devices in a mesh: seq: 8 (over z, y), tensor: 4 (over x, core).
Axes of the slice: x: 2, y: 2, z: 4, core: 2. Of those that a mesh axis runs over, the one named last changes fastest.
Arguments:
- tokens: bfloat16 [2048, 1024], P('seq'), may hold values from -6 to 6
- w_attn: bfloat16 [2, 1024, 3, 1024], P(None, None, None, 'tensor'), may hold values from -0.1875 to 0.1875
- w_out: bfloat16 [2, 1024, 1024], P(None, None, 'tensor'), may hold values from -0.1875 to 0.1875
- w_up: bfloat16 [2, 1024, 4096], P(None, None, 'tensor'), may hold values from -0.1875 to 0.1875
- w_down: bfloat16 [2, 1024, 4096], P(None, None, 'tensor'), may hold values from -0.09375 to 0.09375
- w_head: bfloat16 [256, 1024], replicated, may hold values from -0.1875 to 0.1875
- gains: float32 [5, 1024], replicated, may hold values from 0.1 to 1.9
- q_cotangent: float32 [2048, 256], P('seq'), may hold values from -0.09 to 0.09
- bounds: int32 [8], P('seq'), may hold values from 1 to 256
- resets: int32 [8], P('seq'), may hold values 0 or 1
Outputs:
- q_values: float32 [2048, 256], P('seq')
- grad_attn: float32 [2, 1024, 3, 1024], P(None, 'seq', None, 'tensor')
- grad_out: float32 [2, 1024, 1024], P(None, 'seq', 'tensor')
- grad_up: float32 [2, 1024, 4096], P(None, 'seq', 'tensor')
- grad_down: float32 [2, 1024, 4096], P(None, 'seq', 'tensor')
- grad_head: float32 [256, 1024], P(None, 'seq')
- grad_gains: float32 [5, 1024], P(None, 'seq')
The draws below stay inside these ranges and needn't reach their ends.
All inputs are finite; a program needn't handle non-finite values. No bound on the sum of `resets` on one device may be relied on, other than what follows from the above.
Results may differ from the reference program's by a relative error of at most 0.033.
Values may be sent and summed in bfloat16 or wider, within the bound.
No kernel may reach another device: no remote copies, remote signals or barrier semaphores. Data moves between devices by JAX's collectives and lax.ppermute only.
A program may use at most 128 MiB of HBM per device.

```python
from functools import partial
import jax
import jax.numpy as jnp
from jax import lax

D = 1024
FF = 4096
ACTIONS = 256
LAYERS = 2
SEG = 256
HD = 128
SEGMENTS = 8
TOKENS = 2048


def touch_ends(values, own_key, low, top_value):
    longest = values.shape.index(max(values.shape))
    spots = []
    for shift in (0, 1):
        where = [jax.random.randint(jax.random.fold_in(own_key, axis), (), 0, length) for axis, length in enumerate(values.shape)]
        where[longest] = (where[longest] + shift) % values.shape[longest]
        spots.append(tuple(where))
    return values.at[spots[0]].set(low).at[spots[1]].set(top_value)


def with_spikes(values, stream_key, source, target, parts, factor):
    owner, partner = [(jnp.arange(values.shape[axis_at]) // (values.shape[axis_at] // parts)).reshape([-1 if axis == axis_at else 1 for axis in range(values.ndim)]) for axis_at in (source, target)]
    chosen = jax.random.permutation(stream_key, parts)[partner]
    strong = (owner == chosen) | (owner == (partner + parts // 2) % parts)
    return jnp.where(strong, factor * values, values)


def block_scale(own_key, extent, shards, low, high):
    level = 1.0
    for axis_at, shards_of in shards:
        heights = jax.random.uniform(jax.random.fold_in(jax.random.fold_in(own_key, 6), axis_at), (shards_of,), jnp.float32, low / len(shards), high / len(shards))
        level = level * jnp.repeat(jnp.exp(heights), extent[axis_at] // shards_of).reshape((-1,) + (1,) * (len(extent) - 1 - axis_at))
    return level


def noise(own_key, shape, deviation, most, shards=(), kind=jnp.bfloat16):
    level = block_scale(own_key, shape, shards, -0.22, 0.18) if shards else 1.0
    drawn = jax.random.normal(own_key, shape, jnp.float32) * deviation * level
    return jnp.minimum(jnp.maximum(drawn, -most), most).astype(kind)


def noise_with(stream_key, dims, scale, reach, pieces, heavy, held_as=jnp.bfloat16):
    values = scale * jax.random.normal(stream_key, dims, jnp.float32)
    if pieces:
        values = values * block_scale(stream_key, dims, pieces, -0.22, 0.18)
    return jnp.clip(with_spikes(values, jax.random.fold_in(stream_key, 3), *heavy), -reach, reach).astype(held_as)


def setup_inputs(seed: int = 0) -> dict:
    arg_keys = jax.random.split(jax.random.key(seed), 11)
    return {
        "tokens": noise_with(arg_keys[0], (TOKENS, D), 1.0, 6.0, ((0, 8),), (0, 1, 8, 2.0)),
        "w_attn": noise(arg_keys[1], (LAYERS, D, 3, D), D ** -0.5, 0.1875, ((3, 4),)),
        "w_out": noise(arg_keys[2], (LAYERS, D, D), D ** -0.5, 0.1875, ((2, 4),)),
        "w_up": noise(arg_keys[3], (LAYERS, D, FF), D ** -0.5, 0.1875, ((2, 4),)),
        "w_down": noise(arg_keys[4], (LAYERS, D, FF), FF ** -0.5, 0.09375, ((2, 4),)),
        "w_head": noise(arg_keys[5], (ACTIONS, D), D ** -0.5, 0.1875),
        "gains": jnp.clip(1.0 + 0.18 * jax.random.normal(arg_keys[6], (2 * LAYERS + 1, D), jnp.float32), 0.1, 1.9),
        "q_cotangent": noise(arg_keys[7], (TOKENS, ACTIONS), 0.015625, 0.09, ((0, 8),), jnp.float32),
        "bounds": touch_ends(jax.random.randint(arg_keys[8], (SEGMENTS,), 1, SEG + 1), jax.random.fold_in(arg_keys[8], 1), 1, SEG).astype(jnp.int32),
        "resets": touch_ends((jax.random.randint(arg_keys[9], (SEGMENTS,), 0, 4) < 1).astype(jnp.int32), jax.random.fold_in(arg_keys[9], 1), 0, 1),
    }


epsilon = 1e-06
highest = lax.Precision.HIGHEST

def rms_norm(hidden, gain):
    values = hidden.astype(jnp.float32)
    return values * lax.rsqrt(lax.optimization_barrier(jnp.mean(values * values, axis=-1, keepdims=True)) + epsilon) * gain

def gelu_tanh(up_proj):
    return jax.nn.gelu(up_proj, approximate=True)

def rounded(matrix):
    return lax.optimization_barrier(matrix.astype(jnp.bfloat16)).astype(jnp.float32)

def contract_rows(left, right):
    return lax.dot_general(left, right, (((0,), (0,)), ((), ())), preferred_element_type=jnp.float32)

def contract_cols(left, right):
    return lax.dot_general(left, right, (((1,), (1,)), ((), ())), preferred_element_type=jnp.float32)

def allowed_mask(length, boundary, restart, prior_bound):
    row_ids = lax.broadcasted_iota(jnp.int32, (length, length), 0)
    col_ids = lax.broadcasted_iota(jnp.int32, (length, length), 1)
    before_cut = row_ids < boundary
    own_part = (col_ids <= row_ids) & ((col_ids >= boundary) | before_cut)
    memory_part = before_cut & (restart == 0) & (col_ids >= prior_bound % length)
    return jnp.concatenate([memory_part, own_part], axis=1).astype(jnp.float32)

def project(normed, weights):
    flattened = weights.reshape(weights.shape[0], -1)
    product = jnp.dot(normed, flattened, preferred_element_type=jnp.float32)
    return product.astype(jnp.bfloat16).reshape(normed.shape[0], weights.shape[1], weights.shape[2])

def attend(queries, key_rows, value_rows, allowed):
    scaling = queries.shape[-1] ** (-0.5)
    scores = jnp.einsum('qhd,khd->hqk', queries.astype(jnp.float32), key_rows.astype(jnp.float32), precision=highest) * scaling
    weights = jnp.exp(scores) * allowed[None]
    attn_probs = weights / lax.optimization_barrier(jnp.sum(weights, axis=-1, keepdims=True))
    context = jnp.einsum('hqk,khd->qhd', rounded(attn_probs), value_rows.astype(jnp.float32), precision=highest)
    return (context.astype(jnp.bfloat16), attn_probs)

def attend_back(queries, key_rows, value_rows, attn_probs, d_context):
    scaling = queries.shape[-1] ** (-0.5)
    d_wide = d_context.astype(jnp.float32)
    d_probs = jnp.einsum('qhd,khd->hqk', d_wide, value_rows.astype(jnp.float32), precision=highest)
    d_values = jnp.einsum('hqk,qhd->khd', rounded(attn_probs), d_wide, precision=highest).astype(jnp.bfloat16)
    d_scores = rounded(attn_probs * (d_probs - lax.optimization_barrier(jnp.sum(d_probs * attn_probs, axis=-1, keepdims=True))) * scaling)
    d_queries = jnp.einsum('hqk,khd->qhd', d_scores, key_rows.astype(jnp.float32), precision=highest).astype(jnp.bfloat16)
    d_keys = jnp.einsum('hqk,qhd->khd', d_scores, queries.astype(jnp.float32), precision=highest).astype(jnp.bfloat16)
    return (d_queries, d_keys, d_values)

def layer_forward(hidden, memory, gain_attn, gain_ffn, w_attn, w_out, w_up, w_down, allowed):
    length = hidden.shape[0]
    head_count = w_attn.shape[2] // HD
    normed = rms_norm(hidden, gain_attn).astype(jnp.bfloat16)
    own_proj = project(normed, w_attn)
    mem_proj = project(memory, w_attn[:, 1:])
    queries = own_proj[:, 0].reshape(length, head_count, HD)
    key_rows = jnp.concatenate([mem_proj[:, 0], own_proj[:, 1]], axis=0).reshape(2 * length, head_count, HD)
    value_rows = jnp.concatenate([mem_proj[:, 1], own_proj[:, 2]], axis=0).reshape(2 * length, head_count, HD)
    context, attn_probs = attend(queries, key_rows, value_rows, allowed)
    flat_context = context.reshape(length, -1)
    middle = (hidden.astype(jnp.float32) + contract_cols(flat_context, w_out)).astype(jnp.bfloat16)
    normed_ffn = rms_norm(middle, gain_ffn).astype(jnp.bfloat16)
    up_proj = jnp.dot(normed_ffn, w_up, preferred_element_type=jnp.float32)
    active = gelu_tanh(up_proj).astype(jnp.bfloat16)
    result = (middle.astype(jnp.float32) + contract_cols(active, w_down)).astype(jnp.bfloat16)
    stored = (normed, queries, key_rows, value_rows, attn_probs, flat_context, middle, normed_ffn, up_proj, active)
    return (result, stored)

def layer_backward(hidden, memory, stored, gain_attn, gain_ffn, w_attn, w_out, w_up, w_down, d_result):
    normed, queries, key_rows, value_rows, attn_probs, flat_context, middle, normed_ffn, up_proj, active = stored
    length, features = hidden.shape
    d_ffn = d_result.astype(jnp.bfloat16)
    grad_down = contract_rows(d_ffn, active)
    d_active = jnp.dot(d_ffn, w_down, preferred_element_type=jnp.float32)
    d_upper = jax.vjp(gelu_tanh, up_proj)[1](d_active)[0].astype(jnp.bfloat16)
    grad_up = contract_rows(normed_ffn, d_upper)
    d_normed_ffn = contract_cols(d_upper, w_up)
    d_mid_norm, grad_gain_ffn = jax.vjp(rms_norm, middle.astype(jnp.float32), gain_ffn)[1](d_normed_ffn)
    d_middle = d_result + d_mid_norm
    d_attn = d_middle.astype(jnp.bfloat16)
    grad_out = contract_rows(d_attn, flat_context)
    d_context = jnp.dot(d_attn, w_out, preferred_element_type=jnp.float32).astype(jnp.bfloat16).reshape(queries.shape)
    d_queries, d_keys, d_values = attend_back(queries, key_rows, value_rows, attn_probs, d_context)
    d_own = jnp.stack([d_queries.reshape(length, -1), d_keys[length:].reshape(length, -1), d_values[length:].reshape(length, -1)], axis=1)
    d_mem = jnp.stack([d_keys[:length].reshape(length, -1), d_values[:length].reshape(length, -1)], axis=1)
    grad_attn = contract_rows(normed, d_own.reshape(length, -1)).reshape(w_attn.shape)
    mem_term = contract_rows(memory, d_mem.reshape(length, -1)).reshape(features, 2, -1)
    grad_attn = grad_attn.at[:, 1:].add(mem_term)
    d_normed = contract_cols(d_own.reshape(length, -1), w_attn.reshape(features, -1))
    d_hid_norm, grad_gain_attn = jax.vjp(rms_norm, hidden.astype(jnp.float32), gain_attn)[1](d_normed)
    return (d_middle + d_hid_norm, (grad_attn, grad_out, grad_up, grad_down), (grad_gain_attn, grad_gain_ffn))

def advance(params, layer_idx, operands):
    w_attn, w_out, w_up, w_down, w_head, gains = params
    seg_hidden, seg_memory, allowed = operands
    return layer_forward(seg_hidden, seg_memory, gains[2 * layer_idx], gains[2 * layer_idx + 1], w_attn[layer_idx], w_out[layer_idx], w_up[layer_idx], w_down[layer_idx], allowed)[0]

def segment_grads(params, totals, operands):
    w_attn, w_out, w_up, w_down, w_head, gains = params
    seg_inputs, seg_memories, allowed, seg_cotangent, top_hidden = operands
    stores = []
    for layer_idx in range(LAYERS):
        stores.append(layer_forward(seg_inputs[layer_idx], seg_memories[layer_idx], gains[2 * layer_idx], gains[2 * layer_idx + 1], w_attn[layer_idx], w_out[layer_idx], w_up[layer_idx], w_down[layer_idx], allowed)[1])
    final_norm = rms_norm(top_hidden, gains[2 * LAYERS]).astype(jnp.bfloat16)
    d_actions = seg_cotangent.astype(jnp.bfloat16)
    grad_head = contract_rows(d_actions, final_norm)
    d_final = jnp.dot(d_actions, w_head, preferred_element_type=jnp.float32)
    d_hidden, grad_gain_top = jax.vjp(rms_norm, top_hidden.astype(jnp.float32), gains[2 * LAYERS])[1](d_final)
    layer_grads = [None] * LAYERS
    gain_grads = [None] * (2 * LAYERS)
    for layer_idx in reversed(range(LAYERS)):
        d_hidden, layer_grads[layer_idx], gain_pair = layer_backward(seg_inputs[layer_idx], seg_memories[layer_idx], stores[layer_idx], gains[2 * layer_idx], gains[2 * layer_idx + 1], w_attn[layer_idx], w_out[layer_idx], w_up[layer_idx], w_down[layer_idx], d_hidden)
        gain_grads[2 * layer_idx] = gain_pair[0]
        gain_grads[2 * layer_idx + 1] = gain_pair[1]
    stacked = [jnp.stack([layer_grads[level_idx][member] for level_idx in range(LAYERS)]) for member in range(4)]
    updated = (totals[0] + stacked[0], totals[1] + stacked[1], totals[2] + stacked[2], totals[3] + stacked[3], totals[4] + grad_head, totals[5] + jnp.stack(gain_grads + [grad_gain_top]))
    return (updated, None)

def reference(tokens, w_attn, w_out, w_up, w_down, w_head, gains, q_cotangent, bounds, resets):
    segments = bounds.shape[0]
    length = tokens.shape[0] // segments
    features = tokens.shape[1]
    params = (w_attn, w_out, w_up, w_down, w_head, gains)
    first_flag = (jnp.arange(segments, dtype=jnp.int32) == 0).astype(jnp.int32)
    restarts = jnp.maximum(resets, first_flag)
    prior_bounds = jnp.roll(bounds, 1)
    masks = lax.map(lambda flags: allowed_mask(length, flags[0], flags[1], flags[2]), (bounds, restarts, prior_bounds))
    hidden = tokens.reshape(segments, length, features)
    layer_inputs = []
    layer_memories = []
    for layer_idx in range(LAYERS):
        memory = jnp.roll(rms_norm(hidden, gains[2 * layer_idx]).astype(jnp.bfloat16), 1, axis=0)
        memory = memory.at[0].set(jnp.zeros((length, features), jnp.bfloat16))
        layer_inputs.append(hidden)
        layer_memories.append(memory)
        hidden = lax.map(partial(advance, params, layer_idx), (hidden, memory, masks))
    final_norm = rms_norm(hidden, gains[2 * LAYERS]).astype(jnp.bfloat16)
    q_values = contract_cols(final_norm.reshape(-1, features), w_head)
    start = (jnp.zeros(w_attn.shape, jnp.float32), jnp.zeros(w_out.shape, jnp.float32), jnp.zeros(w_up.shape, jnp.float32), jnp.zeros(w_down.shape, jnp.float32), jnp.zeros(w_head.shape, jnp.float32), jnp.zeros(gains.shape, jnp.float32))
    operands = (tuple(layer_inputs), tuple(layer_memories), masks, q_cotangent.reshape(segments, length, -1), hidden)
    totals, _ = lax.scan(partial(segment_grads, params), start, operands)
    return (q_values, totals[0], totals[1], totals[2], totals[3], totals[4], totals[5])
```

```python
import functools

import jax
import jax.numpy as jnp
from jax import lax
from jax.experimental import pallas as pl
from jax.experimental.pallas import tpu as pltpu
from jax.sharding import PartitionSpec as P

F32 = jnp.float32
BF = jnp.bfloat16
HD = 128
LANES = 128
EPS = 1e-06
GELU_C = (2.0 / jnp.pi) ** 0.5
GELU_A = 0.044715


def nn(left, right):
    return lax.dot_general(left, right, (((1,), (0,)), ((), ())), preferred_element_type=F32)


def nt(left, right):
    return lax.dot_general(left, right, (((1,), (1,)), ((), ())), preferred_element_type=F32)


def tn(left, right):
    return lax.dot_general(left, right, (((0,), (0,)), ((), ())), preferred_element_type=F32)


def shape(dims, kind):
    return jax.ShapeDtypeStruct(tuple(dims), kind)


def whole(dims):
    return pl.BlockSpec(tuple(dims), lambda *_: (0,) * len(dims))


def smem():
    return pl.BlockSpec(memory_space=pltpu.SMEM)


def both(first, second):
    return jnp.concatenate([first[...], second[...]], axis=0)


def inverse_rms(values):
    return lax.rsqrt(jnp.mean(values * values, axis=-1, keepdims=True) + EPS)


def norm_first_kernel(meta, tokens, gains, h_own, a_own, a_oth):
    half = h_own.shape[0]
    core = meta[2]
    for part, target in ((core, a_own), (1 - core, a_oth)):
        rows = tokens[pl.ds(pl.multiple_of(part * half, half), half), :]
        if target is a_own:
            h_own[...] = rows
        values = rows.astype(F32)
        target[...] = (values * inverse_rms(values) * gains[0:1, :]).astype(BF)


def norm_first(meta, tokens, gains):
    half = tokens.shape[0] // 2
    features = tokens.shape[1]
    dims = (half, features)
    return pl.pallas_call(
        norm_first_kernel,
        in_specs=[smem(), whole(tokens.shape), whole(gains.shape)],
        out_specs=[whole(dims)] * 3,
        grid=(1,),
        out_shape=[shape(dims, BF)] * 3,
        name="norm_first",
    )(meta, tokens, gains)


def norm_next_kernel(row, mine, got, res, gains, h_out, n_out):
    total = mine[...].astype(F32) + got[...].astype(F32)
    hidden = (res[...].astype(F32) + total).astype(BF)
    h_out[...] = hidden
    values = hidden.astype(F32)
    n_out[...] = (values * inverse_rms(values) * gains[row : row + 1, :]).astype(BF)


def norm_next(row, mine, got, res, gains):
    dims = mine.shape
    return pl.pallas_call(
        functools.partial(norm_next_kernel, row),
        in_specs=[whole(dims)] * 3 + [whole(gains.shape)],
        out_specs=[whole(dims)] * 2,
        grid=(1,),
        out_shape=[shape(dims, BF)] * 2,
        name="norm_next",
    )(mine, got, res, gains)


def norm_grad(values, gain, upstream):
    inv = inverse_rms(values)
    scaled = upstream * gain
    unit = values * inv
    d_values = inv * (scaled - unit * jnp.mean(scaled * unit, axis=-1, keepdims=True))
    d_gain = jnp.sum(upstream * unit, axis=0, keepdims=True)
    return d_values, d_gain


def norm_last_kernel(row, mine, got, res, gains, d_final, n_out, dh_out, dy_out, dg_out):
    total = mine[...].astype(F32) + got[...].astype(F32)
    values = (res[...].astype(F32) + total).astype(BF).astype(F32)
    gain = gains[row : row + 1, :]
    n_out[...] = (values * inverse_rms(values) * gain).astype(BF)
    d_values, d_gain = norm_grad(values, gain, d_final[...])
    dh_out[...] = d_values
    dy_out[...] = d_values.astype(BF)
    dg_out[...] = d_gain


def norm_last(row, mine, got, res, gains, d_final):
    dims = mine.shape
    line = (1, dims[1])
    return pl.pallas_call(
        functools.partial(norm_last_kernel, row),
        in_specs=[whole(dims)] * 3 + [whole(gains.shape), whole(dims)],
        out_specs=[whole(dims)] * 3 + [whole(line)],
        grid=(1,),
        out_shape=[shape(dims, BF), shape(dims, F32), shape(dims, BF), shape(line, F32)],
        name="norm_last",
    )(mine, got, res, gains, d_final)


def norm_back_kernel(row, mine, got, hidden, gains, d_prev, dh_out, dy_out, dg_out):
    upstream = mine[...].astype(F32) + got[...].astype(F32)
    d_values, d_gain = norm_grad(hidden[...].astype(F32), gains[row : row + 1, :], upstream)
    d_hidden = d_prev[...] + d_values
    dh_out[...] = d_hidden
    dy_out[...] = d_hidden.astype(BF)
    dg_out[...] = d_gain


def norm_back(row, mine, got, hidden, gains, d_prev):
    dims = mine.shape
    line = (1, dims[1])
    return pl.pallas_call(
        functools.partial(norm_back_kernel, row),
        in_specs=[whole(dims)] * 3 + [whole(gains.shape), whole(dims)],
        out_specs=[whole(dims)] * 2 + [whole(line)],
        grid=(1,),
        out_shape=[shape(dims, F32), shape(dims, BF), shape(line, F32)],
        name="norm_back",
    )(mine, got, hidden, gains, d_prev)


def qkv_kernel(meta, a_own, a_oth, weights, kv_out, q_out):
    step = pl.program_id(0)
    length, cols = q_out.shape
    product = nn(both(a_own, a_oth), weights[0, 0]).astype(BF)

    @pl.when(step == 0)
    def _():
        kv_out[0:length, 0:cols] = product
        kv_out[length:, :] = jnp.full(
            (kv_out.shape[0] - length, kv_out.shape[1]), meta[0], jnp.int32
        ).astype(F32).astype(BF)

    @pl.when(step == 1)
    def _():
        kv_out[0:length, cols:] = product

    @pl.when(step == 2)
    def _():
        q_out[...] = product


def qkv_project(layer, meta, a_own, a_oth, w_attn):
    half, features = a_own.shape
    cols = w_attn.shape[3]
    kv_dims = (2 * half + 16, 2 * cols)
    q_dims = (2 * half, cols)
    return pl.pallas_call(
        qkv_kernel,
        grid=(3,),
        in_specs=[
            smem(),
            whole(a_own.shape),
            whole(a_oth.shape),
            pl.BlockSpec((1, 1, features, cols), lambda i: (layer, lax.rem(i + 1, 3), 0, 0)),
        ],
        out_specs=[whole(kv_dims), whole(q_dims)],
        out_shape=[shape(kv_dims, BF), shape(q_dims, BF)],
        name="qkv_project",
    )(meta, a_own, a_oth, w_attn)


def attend_kernel(meta, q_ref, kv, mem, w_out, part_own, part_oth, ctx_out, p_out):
    length, cols = q_ref.shape
    half = length // 2
    bound, restart, core = meta[0], meta[1], meta[2]
    scale = HD**-0.5
    row_pos = lax.broadcasted_iota(jnp.int32, (length, length), 0) + core * half
    row_pos = jnp.where(row_pos >= length, row_pos - length, row_pos)
    col_pos = lax.broadcasted_iota(jnp.int32, (length, length), 1) + core * half
    col_pos = jnp.where(col_pos >= length, col_pos - length, col_pos)
    before = row_pos < bound
    own_ok = (col_pos <= row_pos) & ((col_pos >= bound) | before)
    prior = mem[length : length + 1, 0:1].astype(F32)
    prior = jnp.where(prior >= float(length), prior - float(length), prior)
    from_row = jnp.where(restart == 0, bound, 0)
    mem_ok = (row_pos < from_row) & (col_pos.astype(F32) >= prior)
    pieces = []
    for head in range(cols // HD):
        cut = slice(head * HD, (head + 1) * HD)
        cut_v = slice(cols + head * HD, cols + (head + 1) * HD)
        q = q_ref[:, cut]
        w_mem = jnp.where(mem_ok, jnp.exp(nt(q, mem[0:length, cut]) * scale), 0.0)
        w_own = jnp.where(own_ok, jnp.exp(nt(q, kv[0:length, cut]) * scale), 0.0)
        total = jnp.sum(w_mem, axis=-1, keepdims=True) + jnp.sum(w_own, axis=-1, keepdims=True)
        inv = 1.0 / total
        p_mem = (w_mem * inv).astype(BF)
        p_own = (w_own * inv).astype(BF)
        p_out[head, :, 0:length] = p_mem
        p_out[head, :, length:] = p_own
        context = nn(p_mem, mem[0:length, cut_v]) + nn(p_own, kv[0:length, cut_v])
        pieces.append(context.astype(BF))
    context = jnp.concatenate(pieces, axis=1)
    ctx_out[...] = context
    product = nt(context, w_out[0]).astype(BF)
    part_own[...] = product[0:half]
    part_oth[...] = product[half:]


def attend(layer, meta, q, kv, mem, w_out):
    length, cols = q.shape
    features = w_out.shape[1]
    half_dims = (length // 2, features)
    p_dims = (cols // HD, length, 2 * length)
    return pl.pallas_call(
        attend_kernel,
        grid=(1,),
        in_specs=[
            smem(),
            whole(q.shape),
            whole(kv.shape),
            whole(mem.shape),
            pl.BlockSpec((1, features, cols), lambda i: (layer, 0, 0)),
        ],
        out_specs=[whole(half_dims)] * 2 + [whole(q.shape), whole(p_dims)],
        out_shape=[shape(half_dims, BF)] * 2 + [shape(q.shape, BF), shape(p_dims, BF)],
        name="attend",
    )(meta, q, kv, mem, w_out)


def ffn_kernel(b_own, b_oth, w_up, w_down, part_own, part_oth, act_out, slope_out, total, rows):
    step = pl.program_id(0)
    half = b_own.shape[0]

    @pl.when(step == 0)
    def _():
        rows[0:half, :] = b_own[...]
        rows[half:, :] = b_oth[...]

    upper = nn(rows[...], w_up[0])
    square = upper * upper
    tanh = jnp.tanh(GELU_C * (upper + GELU_A * (square * upper)))
    cdf = 0.5 * (1.0 + tanh)
    active = (upper * cdf).astype(BF)
    act_out[...] = active
    slope = cdf + 0.5 * upper * (1.0 - tanh * tanh) * (GELU_C * (1.0 + 3.0 * GELU_A * square))
    slope_out[...] = slope.astype(BF)
    product = nt(active, w_down[0])

    @pl.when(step == 0)
    def _():
        total[...] = product

    @pl.when(step > 0)
    def _():
        total[...] += product

    @pl.when(step == pl.num_programs(0) - 1)
    def _():
        part_own[...] = total[0:half, :].astype(BF)
        part_oth[...] = total[half:, :].astype(BF)


def ffn(layer, b_own, b_oth, w_up, w_down, chunk=256):
    half, features = b_own.shape
    units = w_up.shape[2]
    chunk = min(chunk, units)
    length = 2 * half
    weight = pl.BlockSpec((1, features, chunk), lambda i: (layer, 0, i))
    tall = pl.BlockSpec((length, chunk), lambda i: (0, i))
    return pl.pallas_call(
        ffn_kernel,
        grid=(units // chunk,),
        in_specs=[whole(b_own.shape)] * 2 + [weight, weight],
        out_specs=[whole(b_own.shape)] * 2 + [tall, tall],
        out_shape=[shape(b_own.shape, BF)] * 2 + [shape((length, units), BF)] * 2,
        scratch_shapes=[pltpu.VMEM((length, features), F32), pltpu.VMEM((length, features), BF)],
        name="ffn",
    )(b_own, b_oth, w_up, w_down)


def head_grad_kernel(meta, cotangent, w_head, dq_own, dq_oth, d_final):
    half = d_final.shape[0]
    core = meta[2]
    own = cotangent[pl.ds(pl.multiple_of(core * half, half), half), :].astype(BF)
    oth = cotangent[pl.ds(pl.multiple_of((1 - core) * half, half), half), :].astype(BF)
    dq_own[...] = own
    dq_oth[...] = oth
    d_final[...] = nn(own, w_head[...])


def head_grad(meta, cotangent, w_head):
    half = cotangent.shape[0] // 2
    actions, features = w_head.shape
    return pl.pallas_call(
        head_grad_kernel,
        grid=(1,),
        in_specs=[smem(), whole(cotangent.shape), whole(w_head.shape)],
        out_specs=[whole((half, actions))] * 2 + [whole((half, features))],
        out_shape=[shape((half, actions), BF)] * 2 + [shape((half, features), F32)],
        name="head_grad",
    )(meta, cotangent, w_head)


def head_values_kernel(meta, f_own, f_oth, w_head, q_out):
    half = f_own.shape[0]
    core = meta[2]
    q_out[pl.ds(pl.multiple_of(core * half, half), half), :] = nt(f_own[...], w_head[...])
    q_out[pl.ds(pl.multiple_of((1 - core) * half, half), half), :] = nt(f_oth[...], w_head[...])


def head_values(meta, f_own, f_oth, w_head):
    dims = (2 * f_own.shape[0], w_head.shape[0])
    return pl.pallas_call(
        head_values_kernel,
        grid=(1,),
        in_specs=[smem(), whole(f_own.shape), whole(f_oth.shape), whole(w_head.shape)],
        out_specs=whole(dims),
        out_shape=shape(dims, F32),
        name="head_values",
    )(meta, f_own, f_oth, w_head)


def ffn_back_kernel(dy_own, dy_oth, slope, w_down, w_up, part_own, part_oth, du_out, total, rows):
    step = pl.program_id(0)
    half = dy_own.shape[0]

    @pl.when(step == 0)
    def _():
        rows[0:half, :] = dy_own[...]
        rows[half:, :] = dy_oth[...]

    d_upper = (nn(rows[...], w_down[0]) * slope[...].astype(F32)).astype(BF)
    du_out[...] = d_upper
    product = nt(d_upper, w_up[0])

    @pl.when(step == 0)
    def _():
        total[...] = product

    @pl.when(step > 0)
    def _():
        total[...] += product

    @pl.when(step == pl.num_programs(0) - 1)
    def _():
        part_own[...] = total[0:half, :].astype(BF)
        part_oth[...] = total[half:, :].astype(BF)


def ffn_back(layer, dy_own, dy_oth, slope, w_down, w_up, chunk=256):
    half, features = dy_own.shape
    units = w_up.shape[2]
    chunk = min(chunk, units)
    length = 2 * half
    weight = pl.BlockSpec((1, features, chunk), lambda i: (layer, 0, i))
    tall = pl.BlockSpec((length, chunk), lambda i: (0, i))
    return pl.pallas_call(
        ffn_back_kernel,
        grid=(units // chunk,),
        in_specs=[whole(dy_own.shape)] * 2 + [tall, weight, weight],
        out_specs=[whole(dy_own.shape)] * 2 + [tall],
        out_shape=[shape(dy_own.shape, BF)] * 2 + [shape((length, units), BF)],
        scratch_shapes=[pltpu.VMEM((length, features), F32), pltpu.VMEM((length, features), BF)],
        name="ffn_back",
    )(dy_own, dy_oth, slope, w_down, w_up)


def attend_back_kernel(
    do_own, do_oth, q_ref, kv, mem, probs, w_out, w_attn, part_own, part_oth, d_out, m_out
):
    length, cols = q_ref.shape
    half = length // 2
    scale = HD**-0.5
    d_context = nn(both(do_own, do_oth), w_out[0]).astype(BF)
    for head in range(cols // HD):
        cut = slice(head * HD, (head + 1) * HD)
        cut_v = slice(cols + head * HD, cols + (head + 1) * HD)
        dc = d_context[:, cut]
        q = q_ref[:, cut]
        keys = (mem[0:length, cut], kv[0:length, cut])
        values = (mem[0:length, cut_v], kv[0:length, cut_v])
        rounded = (probs[head, :, 0:length], probs[head, :, length:])
        wide = [part.astype(F32) for part in rounded]
        d_probs = [nt(dc, part) for part in values]
        mean = sum(
            jnp.sum(a * b, axis=-1, keepdims=True) for a, b in zip(d_probs, wide, strict=True)
        )
        d_scores = [
            (a * (b - mean) * scale).astype(BF) for a, b in zip(wide, d_probs, strict=True)
        ]
        d_q = nn(d_scores[0], keys[0]) + nn(d_scores[1], keys[1])
        d_out[:, cut] = d_q.astype(BF)
        m_out[:, cut] = tn(d_scores[0], q).astype(BF)
        d_out[:, cut_v] = tn(d_scores[1], q).astype(BF)
        m_out[:, cut_v] = tn(rounded[0], dc).astype(BF)
        lane = 2 * cols + head * HD
        d_out[:, lane : lane + HD] = tn(rounded[1], dc).astype(BF)
    product = nt(d_out[:, 0:cols], w_attn[0, 0])
    product += nt(d_out[:, cols : 2 * cols], w_attn[0, 1])
    product += nt(d_out[:, 2 * cols :], w_attn[0, 2])
    part_own[...] = product[0:half].astype(BF)
    part_oth[...] = product[half:].astype(BF)


def attend_back(layer, do_own, do_oth, q, kv, mem, probs, w_out, w_attn):
    length, cols = q.shape
    features = w_out.shape[1]
    half_dims = do_own.shape
    d_dims = (length, 3 * cols)
    m_dims = (length, 2 * cols)
    return pl.pallas_call(
        attend_back_kernel,
        grid=(1,),
        in_specs=[whole(half_dims)] * 2
        + [whole(q.shape), whole(kv.shape), whole(mem.shape), whole(probs.shape)]
        + [
            pl.BlockSpec((1, features, cols), lambda i: (layer, 0, 0)),
            pl.BlockSpec((1, 3, features, cols), lambda i: (layer, 0, 0, 0)),
        ],
        out_specs=[whole(half_dims)] * 2 + [whole(d_dims), whole(m_dims)],
        out_shape=[shape(half_dims, BF)] * 2 + [shape(d_dims, BF), shape(m_dims, BF)],
        name="attend_back",
    )(do_own, do_oth, q, kv, mem, probs, w_out, w_attn)


def owner_of(place, stages):
    bits = len(stages)
    owner = 0
    for at, stage in enumerate(stages):
        owner = owner + stage * lax.rem(lax.div(place, 1 << (bits - 1 - at)), 2)
    return owner


def weight_grad(name, terms, group, stages):
    half, features = terms[0][0][0].shape
    count = 1 << len(stages)
    rows = features // count
    width = max(column + term[1].shape[-1] for *term, column in terms)
    columns = sorted({column for *_, column in terms})
    lefts, rights, plan = [], [], []
    for left, right, column in terms:
        at_left = [id(entry[0]) for entry in lefts]
        if id(left[0]) not in at_left:
            lefts.append(left)
            at_left.append(id(left[0]))
        rights.append(right)
        plan.append((at_left.index(id(left[0])), column))

    def body(group_ref, *refs):
        step = pl.program_id(0)
        send, keep = refs[-2], refs[-1]
        left_values = [
            both(refs[2 * k], refs[2 * k + 1]) for k in range(len(lefts))
        ]
        parts = []
        for column in columns:
            product = None
            for k, (at, where) in enumerate(plan):
                if where == column:
                    piece = tn(left_values[at], refs[2 * len(lefts) + k][...])
                    product = piece if product is None else add_to(product, piece)
            parts.append((column, product))
        for target, wanted in ((send, step < count // 2), (keep, step >= count // 2)):

            @pl.when(wanted)
            def _():
                for column, product in parts:
                    target[:, column : column + product.shape[1]] = product.astype(BF)

    def add_to(product, piece):
        if piece.shape == product.shape:
            return product + piece
        start = product.shape[1] - piece.shape[1]
        return jnp.concatenate([product[:, :start], product[:, start:] + piece], axis=1)

    half_count = count // 2

    def left_index(i, group_ref):
        place = lax.rem(i + half_count, count)
        return (0, owner_of(place, stages) ^ group_ref[0])

    left_spec = pl.BlockSpec((half, rows), left_index)
    out_dims = (features // 2, width)
    return pl.pallas_call(
        body,
        grid_spec=pltpu.PrefetchScalarGridSpec(
            num_scalar_prefetch=1,
            grid=(count,),
            in_specs=[left_spec] * (2 * len(lefts)) + [whole(right.shape) for right in rights],
            out_specs=[
                pl.BlockSpec((rows, width), lambda i, g: (jnp.minimum(i, half_count - 1), 0)),
                pl.BlockSpec((rows, width), lambda i, g: (jnp.maximum(i - half_count, 0), 0)),
            ],
        ),
        out_shape=[shape(out_dims, BF)] * 2,
        name=name,
    )(group, *[piece for left in lefts for piece in left], *rights)


def split_kernel(keep_low, keep_high, got_low, got_high, send, keep):
    send[...] = (keep_high[...].astype(F32) + got_high[...].astype(F32)).astype(BF)
    keep[...] = (keep_low[...].astype(F32) + got_low[...].astype(F32)).astype(BF)


def split_sum(keep, got):
    rows, width = keep.shape
    rows = rows // 2
    block = min(rows, 128)
    steps = rows // block
    low = pl.BlockSpec((block, width), lambda i: (i, 0))
    high = pl.BlockSpec((block, width), lambda i: (i + steps, 0))
    return pl.pallas_call(
        split_kernel,
        grid=(steps,),
        in_specs=[low, high, low, high],
        out_specs=[low, low],
        out_shape=[shape((rows, width), BF)] * 2,
        name="split_sum",
    )(keep, keep, got, got)


def scatter_sum(send, keep, stages, stride):
    for at, stage in enumerate(stages):
        got = swap(send, "seq", stage * stride)
        if at + 1 < len(stages):
            send, keep = split_sum(keep, got)
    return keep, got


def plain_pair_kernel(k_first, g_first, k_second, g_second, out):
    out[0] = k_first[...].astype(F32) + g_first[...].astype(F32)
    out[1] = k_second[...].astype(F32) + g_second[...].astype(F32)


def plain_pair(first, second):
    dims = first[0].shape
    return pl.pallas_call(
        plain_pair_kernel,
        grid=(1,),
        in_specs=[whole(dims)] * 4,
        out_specs=whole((2,) + dims),
        out_shape=shape((2,) + dims, F32),
        name="plain_pair",
    )(*first, *second)


def attn_pair_kernel(k_first, g_first, k_second, g_second, attn, out, head):
    cols = attn.shape[3]
    for layer, (keep, got) in enumerate(((k_first, g_first), (k_second, g_second))):
        total = keep[...].astype(F32) + got[...].astype(F32)
        for which in range(3):
            attn[layer, which] = total[:, which * cols : (which + 1) * cols]
        out[layer] = total[:, 3 * cols : 4 * cols]
        if layer == 1:
            head[...] = total[:, 4 * cols :].T


def attn_pair(first, second, cols):
    rows = first[0].shape[0]
    actions = second[0].shape[1] - 4 * cols
    dims = [(2, 3, rows, cols), (2, rows, cols), (actions, rows)]
    return pl.pallas_call(
        attn_pair_kernel,
        grid=(1,),
        in_specs=[whole(first[0].shape)] * 2 + [whole(second[0].shape)] * 2,
        out_specs=[whole(dim) for dim in dims],
        out_shape=[shape(dim, F32) for dim in dims],
        name="attn_pair",
    )(*first, *second)


def swap(value, axis, mask):
    count = lax.axis_size(axis)
    return lax.ppermute(value, axis, [(source, source ^ mask) for source in range(count)])


def shifted(value, axis, steps):
    count = lax.axis_size(axis)
    initial, last = (max(0, -steps), min(count, count - steps))
    return lax.ppermute(value, axis, [(source, source + steps) for source in range(initial, last)])


def add_bf16(left, right):
    return (left.astype(F32) + right.astype(F32)).astype(BF)


def half_total(part_own, part_oth):
    mine = add_bf16(part_own, swap(part_oth, "tensor", 1))
    mask = 2
    while True:
        got = swap(mine, "tensor", mask)
        mask *= 2
        if mask >= lax.axis_size("tensor"):
            return mine, got
        mine = add_bf16(mine, got)


def body(tokens, w_attn, w_out, w_up, w_down, w_head, gains, q_cotangent, bounds, resets):
    layers = w_attn.shape[0]
    features = tokens.shape[1]
    cols = w_attn.shape[3]
    seq_count = lax.axis_size("seq")
    seq_at = lax.axis_index("seq")
    core = lax.axis_index("tensor") % 2
    groups = min(seq_count, features // LANES)
    stride = seq_count // groups
    stages = [1 << bit for bit in range(groups.bit_length() - 1)]
    group = (seq_at // stride).astype(jnp.int32).reshape(1)
    restart = jnp.where(seq_at == 0, 1, resets[0])
    meta = jnp.stack([bounds[0], restart, core]).astype(jnp.int32)
    w_attn = jnp.transpose(w_attn, (0, 2, 1, 3))

    hidden, a_own, a_oth = norm_first(meta, tokens, gains)
    dq_own, dq_oth, d_final = head_grad(meta, q_cotangent, w_head)
    stores = []
    for layer in range(layers):
        kv, q = qkv_project(layer, meta, a_own, a_oth, w_attn)
        mem = shifted(kv, "seq", 1)
        part_own, part_oth, context, probs = attend(layer, meta, q, kv, mem, w_out)
        mine, got = half_total(part_own, part_oth)
        middle, b_own = norm_next(2 * layer + 1, mine, got, hidden, gains)
        b_oth = swap(b_own, "tensor", 1)
        part_own, part_oth, active, slope = ffn(layer, b_own, b_oth, w_up, w_down)
        mine, got = half_total(part_own, part_oth)
        stores.append(
            (hidden, a_own, a_oth, q, kv, mem, probs, context, middle, b_own, b_oth, active, slope)
        )
        if layer + 1 < layers:
            hidden, a_own = norm_next(2 * layer + 2, mine, got, middle, gains)
            a_oth = swap(a_own, "tensor", 1)
    f_own, d_hidden, dy_own, d_gain = norm_last(2 * layers, mine, got, middle, gains, d_final)
    dy_oth = swap(dy_own, "tensor", 1)
    f_oth = swap(f_own, "tensor", 1)
    q_values = head_values(meta, f_own, f_oth, w_head)

    gain_grads = {2 * layers: d_gain}
    grads = {}
    for layer in reversed(range(layers)):
        hidden, a_own, a_oth, q, kv, mem, probs, context, middle, b_own, b_oth, active, slope = (
            stores[layer]
        )
        part_own, part_oth, d_upper = ffn_back(layer, dy_own, dy_oth, slope, w_down, w_up)
        sent = weight_grad("grad_down", [((dy_own, dy_oth), active, 0)], group, stages)
        grads["down", layer] = scatter_sum(*sent, stages, stride)
        sent = weight_grad("grad_up", [((b_own, b_oth), d_upper, 0)], group, stages)
        grads["up", layer] = scatter_sum(*sent, stages, stride)
        mine, got = half_total(part_own, part_oth)
        d_hidden, do_own, gain_grads[2 * layer + 1] = norm_back(
            2 * layer + 1, mine, got, middle, gains, d_hidden
        )
        do_oth = swap(do_own, "tensor", 1)
        part_own, part_oth, d_own, d_mem = attend_back(
            layer, do_own, do_oth, q, kv, mem, probs, w_out, w_attn
        )
        returned = shifted(d_mem, "seq", -1)
        terms = [
            ((a_own, a_oth), d_own, 0),
            ((a_own, a_oth), returned, 0),
            ((do_own, do_oth), context, 3 * cols),
        ]
        if layer == layers - 1:
            d_actions = jnp.concatenate([dq_own, dq_oth], axis=0)
            terms.append(((f_own, f_oth), d_actions, 4 * cols))
        sent = weight_grad("grad_attn", terms, group, stages)
        grads["attn", layer] = scatter_sum(*sent, stages, stride)
        mine, got = half_total(part_own, part_oth)
        d_hidden, dy_own, gain_grads[2 * layer] = norm_back(
            2 * layer, mine, got, hidden, gains, d_hidden
        )
        if layer > 0:
            dy_oth = swap(dy_own, "tensor", 1)

    grad_down = plain_pair(*[grads["down", layer] for layer in range(layers)])
    grad_up = plain_pair(*[grads["up", layer] for layer in range(layers)])
    grad_attn, grad_out, grad_head = attn_pair(*[grads["attn", layer] for layer in range(layers)], cols)
    grad_gains = jnp.concatenate([gain_grads[row] for row in range(2 * layers + 1)], axis=0)
    grad_gains = grad_gains + swap(grad_gains, "tensor", 1)
    for stage in stages:
        grad_gains = grad_gains + swap(grad_gains, "seq", stage * stride)
    grad_gains = lax.dynamic_slice_in_dim(grad_gains, group[0] * (features // groups), features // groups, 1)
    if stride > 1:
        lines = [list(range(first, first + stride)) for first in range(0, seq_count, stride)]
        scatter = functools.partial(
            lax.psum_scatter, axis_name="seq", axis_index_groups=lines, tiled=True
        )
        grad_attn = scatter(grad_attn, scatter_dimension=2)
        grad_out = scatter(grad_out, scatter_dimension=1)
        grad_up = scatter(grad_up, scatter_dimension=1)
        grad_down = scatter(grad_down, scatter_dimension=1)
        grad_head = scatter(grad_head, scatter_dimension=1)
        grad_gains = scatter(grad_gains, scatter_dimension=1)
    grad_attn = jnp.transpose(grad_attn, (0, 2, 1, 3))
    return (q_values, grad_attn, grad_out, grad_up, grad_down, grad_head, grad_gains)


def solution(mesh):
    placed = (
        P("seq", None),
        P(None, None, None, "tensor"),
        P(None, None, "tensor"),
        P(None, None, "tensor"),
        P(None, None, "tensor"),
        P(),
        P(),
        P("seq", None),
        P("seq"),
        P("seq"),
    )
    return jax.shard_map(
        body,
        mesh=mesh,
        in_specs=placed,
        out_specs=(
            P("seq", None),
            P(None, "seq", None, "tensor"),
            P(None, "seq", "tensor"),
            P(None, "seq", "tensor"),
            P(None, "seq", "tensor"),
            P(None, "seq"),
            P(None, "seq"),
        ),
        check_vma=False,
    )
```
